32 devices in a mesh: dp: 8 (over y, x, core), own: 4 (over z).
Axes of the slice: x: 2, y: 2, z: 4, core: 2. Of those that a mesh axis runs over, the one named last changes fastest.
Arguments:
- grads: bfloat16 [8, 6, 8192, 128], P('dp', None, 'own'), may hold values from -6 to 6
- proj: bfloat16 [4, 3, 8192, 1024], P('own', None, 'dp'), may hold values from -0.0625 to 0.0625
- moment1: float32 [4, 3, 1024, 128], P('own', None, 'dp'), may hold values from -24 to 24
- moment2: float32 [4, 3, 1024, 128], P('own', None, 'dp'), may hold values from 0.05 to 5
- plan: int32 [6], replicated, may hold values from 0 to 3, as said below
Outputs:
- update: bfloat16 [6, 8192, 128], P(None, 'own')
- new_moment1: float32 [4, 3, 1024, 128], P('own', None, 'dp')
- new_moment2: float32 [4, 3, 1024, 128], P('own', None, 'dp')
The draws below stay inside these ranges and needn't reach their ends.
Inputs may be any that keep to these rules, and one draw needn't show every extreme that they name: `plan`: no owner is named more than 3 times, and some owner is named exactly 3 times.
All inputs are finite; a program needn't handle non-finite values.
Results may differ from the reference program's by a relative error of at most 0.015.
Values may be sent and summed in bfloat16 or wider, within the bound.
A program may use at most 64 MiB of HBM per device.

```python
import math
import jax
import jax.numpy as jnp
from jax import lax

D = 8192
RANK = 1024
COLS = 128
CAP = 3
MATS = 6
N_DP = 8
N_OWN = 4


def draw_plan(key, part):
    places = N_OWN * CAP
    key_score, key_full, key_order = jax.random.split(key, 3)
    scores = jax.random.randint(key_score, (places,), 0, 1000)
    favored = jax.random.randint(key_full, (), 0, N_OWN)
    owners = jnp.arange(places, dtype=jnp.int32) // CAP
    ranked = scores * places + jnp.arange(places, dtype=jnp.int32) + jnp.where(owners == favored, 1000 * places, 0)
    chosen = jnp.argsort(-ranked, stable=True)[:MATS]
    picked = owners[chosen]
    shuffle = jax.random.permutation(key_order, MATS)
    return picked[shuffle].astype(jnp.int32)


def block_levels(stream_key, extent, pieces, low, high):
    def one(axis_at, blocks):
        heights = jax.random.uniform(jax.random.fold_in(jax.random.fold_in(stream_key, 6), axis_at), (blocks,), jnp.float32, low / len(pieces), high / len(pieces))
        return jnp.repeat(jnp.exp(heights), extent[axis_at] // blocks).reshape((-1,) + (1,) * (len(extent) - axis_at - 1))

    level = one(*pieces[0])
    for cut in pieces[1:]:
        level = level * one(*cut)
    return level


def scatter_about(stream_key, dims, scale, limit, pieces=(), kind=jnp.bfloat16):
    array = jax.random.normal(stream_key, dims, jnp.float32) * scale
    if len(pieces) > 0:
        array = block_levels(stream_key, dims, pieces, -0.22, 0.18) * array
    return jnp.clip(array, min=-limit, max=limit).astype(kind)


def setup_inputs(seed: int = 0) -> dict:
    key_list = jax.random.split(jax.random.key(seed), 6)
    return {
        "grads": scatter_about(key_list[0], (N_DP, MATS, D, COLS), 1.0, 6.0, ((0, 8), (2, 4))),
        "proj": scatter_about(key_list[1], (N_OWN, CAP, D, RANK), D ** -0.5, 0.0625, ((0, 4), (2, 8))),
        "moment1": scatter_about(key_list[2], (N_OWN, CAP, RANK, COLS), 4.0, 24.0, ((0, 4), (2, 8)), jnp.float32),
        "moment2": jnp.clip(jnp.exp(math.log(5.0) - 4.6051702 * jax.random.uniform(key_list[3], (N_OWN, CAP, RANK, COLS), jnp.float32) ** block_levels(key_list[3], (N_OWN, CAP, RANK, COLS), ((0, 4), (2, 8)), -0.2, 0.2)), 0.05, 5.0),
        "plan": draw_plan(jax.random.fold_in(key_list[5], 71), 0),
    }


beta_one = 0.9
beta_two = 0.999
adam_eps = 1e-08
norm_eps = 1e-06
correct_one = 1.0 - 0.9 ** 10
correct_two = 1.0 - 0.999 ** 10

def slot_selector(plan):
    matrices = plan.shape[0]
    places = jnp.arange(N_OWN * CAP, dtype=jnp.int32)
    owners = places // CAP
    within = places % CAP
    index = jnp.arange(matrices, dtype=jnp.int32)
    before = lax.optimization_barrier(jnp.sum(((plan[None, :] == plan[:, None]) & (index[None, :] < index[:, None])).astype(jnp.int32), axis=1))
    chosen = (plan[None, :] == owners[:, None]) & (before[None, :] == within[:, None])
    return chosen.astype(jnp.float32)

def reference(grads, proj, moment1, moment2, plan):
    selector = slot_selector(plan)
    total = lax.optimization_barrier(jnp.sum(grads.astype(jnp.float32), axis=0))
    slot_grad = jnp.einsum('sj,jdc->sdc', selector, total)
    grad_half = lax.optimization_barrier(slot_grad.astype(jnp.bfloat16))
    projection = proj.reshape(N_OWN * CAP, D, RANK).astype(jnp.float32)
    rank_grad = jnp.einsum('sdr,sdc->src', projection, grad_half.astype(jnp.float32))
    first_old = moment1.reshape(N_OWN * CAP, RANK, COLS)
    second_old = moment2.reshape(N_OWN * CAP, RANK, COLS)
    first_new = beta_one * first_old + (1.0 - beta_one) * rank_grad
    second_new = beta_two * second_old + (1.0 - beta_two) * rank_grad * rank_grad
    adam_step = first_new / correct_one / (jnp.sqrt(second_new / correct_two) + adam_eps)
    adam_half = lax.optimization_barrier(adam_step.astype(jnp.bfloat16)).astype(jnp.float32)
    rank_half = lax.optimization_barrier(rank_grad.astype(jnp.bfloat16)).astype(jnp.float32)
    grad_norms = lax.optimization_barrier(jnp.sum(rank_grad * rank_grad, axis=1))
    step_norms = lax.optimization_barrier(jnp.sum(adam_half * adam_half, axis=1))
    column_scale = jnp.sqrt(step_norms) / (jnp.sqrt(grad_norms) + norm_eps)
    combined = lax.optimization_barrier((adam_half - column_scale[:, None, :] * rank_half).astype(jnp.bfloat16))
    slot_update = jnp.einsum('sdr,src->sdc', projection, combined.astype(jnp.float32)) + column_scale[:, None, :] * slot_grad
    update_half = lax.optimization_barrier(slot_update.astype(jnp.bfloat16))
    update = jnp.einsum('sj,sdc->jdc', selector, update_half.astype(jnp.float32)).astype(jnp.bfloat16)
    return (update, first_new.reshape(N_OWN, CAP, RANK, COLS), second_new.reshape(N_OWN, CAP, RANK, COLS))
```

```python
import functools
import jax
import jax.numpy as jnp
from jax import lax
from jax.experimental import pallas as pl
from jax.experimental.pallas import tpu as pltpu
from jax.sharding import PartitionSpec as P

beta_one = 0.9
beta_two = 0.999
adam_eps = 1e-08
norm_eps = 1e-06
correct_one = 1.0 - 0.9**10
correct_two = 1.0 - 0.999**10

CHUNKS = 2
F32 = jnp.float32
BF16 = jnp.bfloat16


def kernel(
    n, m, plan, grads, proj, m1, m2, out, m1_out, m2_out,
    own_half, pair_half, half_sum, chip_in, total, slot_out, slot_in, grad, weights,
    part, part_in, pair_sum, share_in, norms, norms_in, mixed, update, row_in, plane_in, picked,
    local_sem,
    s_pair, r_pair, s_chip, r_chip, s_slot, r_slot, s_row, r_row,
    s_part, r_part, s_share, r_share, s_norm, r_norm, s_mix, r_mix, s_mixf, r_mixf,
    s_back, r_back, s_home, r_home, s_out, r_out, s_outf, r_outf,
):
    mats = grads.shape[0]
    chips = n // 2
    piece = grads.shape[3]
    chunk = piece // CHUNKS
    cap = m1.shape[0]
    rank_rows = m1.shape[1]
    cols = m1.shape[2]
    rank = n * rank_rows
    dp = lax.axis_index("dp")
    own = lax.axis_index("own")
    core = lax.rem(dp, 2)
    chip = lax.div(dp, 2)
    other = 1 - core
    partner = (2 * chip + other, own)

    def at_chip(which):
        return (2 * which + core, own)

    def remote(src, dst, send, recv, device):
        return pltpu.make_async_remote_copy(
            src_ref=src, dst_ref=dst, send_sem=send, recv_sem=recv,
            device_id=device, device_id_type=pl.DeviceIdType.MESH,
        )

    def rows(ch):
        return pl.ds(ch * chunk, chunk)

    load_half = pltpu.make_async_copy(grads.at[:, core], own_half, local_sem.at[0])
    load_half.start()
    load_proj = pltpu.make_async_copy(proj, weights, local_sem.at[1])
    load_proj.start()

    owner = [plan[j] for j in range(mats)]
    place = []
    for j in range(mats):
        before = jnp.int32(0)
        for i in range(j):
            before = before + jnp.where(owner[i] == owner[j], 1, 0)
        place.append(owner[j] * cap + before)

    def occupant(slot):
        index = jnp.int32(0)
        valid = jnp.int32(0)
        for j in range(mats):
            here = place[j] == slot
            index = jnp.where(here, j, index)
            valid = jnp.where(here, 1, valid)
        return index, valid.astype(F32)

    barrier = pltpu.get_barrier_semaphore()
    for d in range(1, n):
        pl.semaphore_signal(
            barrier, inc=1, device_id=(lax.rem(dp + d, n), own),
            device_id_type=pl.DeviceIdType.MESH,
        )
    for d in range(1, m):
        pl.semaphore_signal(
            barrier, inc=1, device_id=(dp, lax.rem(own + d, m)),
            device_id_type=pl.DeviceIdType.MESH,
        )
    pl.semaphore_wait(barrier, n - 1 + m - 1)

    sends = []

    pair = []
    for ch in range(CHUNKS):
        c = remote(
            grads.at[:, other, :, rows(ch)], pair_half.at[:, :, rows(ch)],
            s_pair.at[ch], r_pair.at[ch], partner,
        )
        c.start()
        pair.append(c)
    load_half.wait()
    over_chips = {}
    for ch in range(CHUNKS):
        pair[ch].wait_recv()

        @pl.loop(0, mats * chips)
        def _(i):
            j = lax.div(i, chips)
            t = lax.rem(i, chips)
            half_sum[t, j, rows(ch)] = (
                own_half[j, t, rows(ch)].astype(F32) + pair_half[j, t, rows(ch)].astype(F32)
            ).astype(BF16)

        for d in range(1, chips):
            to = lax.rem(chip + d, chips)
            c = remote(
                half_sum.at[to, :, rows(ch)], chip_in.at[d - 1, :, rows(ch)],
                s_chip.at[ch, d], r_chip.at[ch, d], at_chip(to),
            )
            c.start()
            over_chips[ch, d] = c
    sends += pair + list(over_chips.values())

    to_owner = {}
    for ch in range(CHUNKS):
        for d in range(1, chips):
            over_chips[ch, d].wait_recv()

        @pl.loop(0, mats)
        def _(j):
            acc = half_sum[chip, j, rows(ch)].astype(F32)
            for d in range(1, chips):
                acc = acc + chip_in[d - 1, j, rows(ch)].astype(F32)
            total[j, rows(ch)] = acc.astype(BF16)

        for dz in list(range(1, m)) + [0]:
            to = lax.rem(own + dz, m)
            for k in range(cap):
                index, valid = occupant(to * cap + k)
                value = (total[index, rows(ch)].astype(F32) * valid).astype(BF16)
                if dz == 0:
                    slot_in[0, k, rows(ch)] = value
                else:
                    slot_out[dz - 1, k, rows(ch)] = value
            if dz > 0:
                c = remote(
                    slot_out.at[dz - 1, :, rows(ch)], slot_in.at[dz, :, rows(ch)],
                    s_slot.at[ch, dz], r_slot.at[ch, dz], (dp, to),
                )
                c.start()
                to_owner[ch, dz] = c
    sends += list(to_owner.values())

    guarded = []
    for ch in range(CHUNKS):
        for dz in range(m):
            if dz > 0:
                to_owner[ch, dz].wait_recv()
            plane = lax.rem(own + m - dz, m)
            d = lax.rem(plane + chips - chip, chips)
            c = remote(
                slot_in.at[dz, :, rows(ch)], grad.at[:, chip, rows(ch)],
                s_row.at[ch, dz], r_row.at[ch, d], at_chip(plane),
            )

            @pl.when(d != 0)
            def _():
                c.start()

            @pl.when(d == 0)
            def _():
                for k in range(cap):
                    grad[k, chip, rows(ch)] = slot_in[dz, k, rows(ch)]

            guarded.append((d, c))
    for ch in range(CHUNKS):
        for d in range(1, chips):
            remote(
                slot_in.at[0, :, rows(ch)], grad.at[:, chip, rows(ch)],
                s_row.at[ch, 0], r_row.at[ch, d], at_chip(chip),
            ).wait_recv()

    load_proj.wait()
    parts = []
    for k in range(cap):
        g = grad[k].reshape(chips * piece, cols)
        w = weights[k].reshape(chips * piece, rank)
        value = lax.dot_general(g, w, (((0,), (0,)), ((), ())), preferred_element_type=F32)
        value = value.T.astype(BF16)
        for t in range(chips):
            for s in range(2):
                at = (2 * t + s) * rank_rows
                part[s, k, t] = value[at : at + rank_rows]
        c = remote(part.at[other, k], part_in.at[k], s_part.at[k], r_part.at[k], partner)
        c.start()
        parts.append(c)
    shares = {}
    for k in range(cap):
        parts[k].wait_recv()
        for t in range(chips):
            pair_sum[k, t] = (part[core, k, t].astype(F32) + part_in[k, t].astype(F32)).astype(BF16)
        for d in range(1, chips):
            to = lax.rem(chip + d, chips)
            c = remote(
                pair_sum.at[k, to], share_in.at[k, d - 1],
                s_share.at[k, d], r_share.at[k, d], at_chip(to),
            )
            c.start()
            shares[k, d] = c
    sends += parts + list(shares.values())

    rank_half = []
    adam = []
    for k in range(cap):
        for d in range(1, chips):
            shares[k, d].wait_recv()
        value = pair_sum[k, chip].astype(F32)
        for d in range(1, chips):
            value = value + share_in[k, d - 1].astype(F32)
        first = beta_one * m1[k] + (1.0 - beta_one) * value
        second = beta_two * m2[k] + (1.0 - beta_two) * value * value
        m1_out[k] = first
        m2_out[k] = second
        step = first / correct_one / (jnp.sqrt(second / correct_two) + adam_eps)
        step = step.astype(BF16)
        wide = step.astype(F32)
        norms[k] = jnp.sum(value * value, axis=0, keepdims=True)
        norms[cap + k] = jnp.sum(wide * wide, axis=0, keepdims=True)
        rank_half.append(value.astype(BF16))
        adam.append(wide)
    across = []
    for d in range(1, n):
        c = remote(
            norms, norms_in.at[d - 1], s_norm.at[d], r_norm.at[d], (lax.rem(dp + d, n), own)
        )
        c.start()
        across.append(c)
    sends += across
    for c in across:
        c.wait_recv()
    sums = norms[...]
    for d in range(1, n):
        sums = sums + norms_in[d - 1]
    scale = []
    for k in range(cap):
        scale.append(jnp.sqrt(sums[cap + k]) / (jnp.sqrt(sums[k]) + norm_eps))
        mixed[k, dp] = (adam[k] - scale[k] * rank_half[k].astype(F32)).astype(BF16)
    mix = []
    for d in range(1, chips):
        to = lax.rem(chip + d, chips)
        c = remote(mixed.at[:, dp], mixed.at[:, dp], s_mix.at[d], r_mix.at[d], at_chip(to))
        c.start()
        mix.append(c)
    forward = []
    c = remote(mixed.at[:, dp], mixed.at[:, dp], s_mixf.at[0], r_mixf.at[0], partner)
    c.start()
    forward.append(c)
    for d in range(1, chips):
        mix[d - 1].wait_recv()
        at = 2 * lax.rem(chip + chips - d, chips) + core
        c = remote(mixed.at[:, at], mixed.at[:, at], s_mixf.at[d], r_mixf.at[d], partner)
        c.start()
        forward.append(c)
    for c in forward:
        c.wait_recv()
    sends += mix + forward

    back = {}
    for ch in range(CHUNKS):
        for k in range(cap):
            w = weights[k, :, rows(ch)].reshape(chips * chunk, rank)
            c_full = mixed[k].reshape(rank, cols)
            value = jnp.dot(w, c_full, preferred_element_type=F32)
            g = grad[k, :, rows(ch)].reshape(chips * chunk, cols).astype(F32)
            value = (value + scale[k] * g).astype(BF16)
            for t in range(chips):
                update[t, k, rows(ch)] = value[t * chunk : (t + 1) * chunk]
        for k in range(cap):
            row_in[chip, k, rows(ch)] = update[chip, k, rows(ch)]
        for d in range(1, chips):
            to = lax.rem(chip + d, chips)
            c = remote(
                update.at[to, :, rows(ch)], row_in.at[chip, :, rows(ch)],
                s_back.at[ch, d], r_back.at[ch, d], at_chip(to),
            )
            c.start()
            back[ch, d] = c
    sends += list(back.values())

    home = {}
    for ch in range(CHUNKS):
        for d in range(1, chips):
            back[ch, d].wait_recv()
        for dz in range(1, m):
            to = lax.rem(own + dz, m)
            c = remote(
                row_in.at[to, :, rows(ch)], plane_in[ch].at[own],
                s_home.at[ch, dz], r_home.at[ch, dz], (dp, to),
            )
            c.start()
            home[ch, dz] = c
        for k in range(cap):
            plane_in[ch][own, k] = row_in[own, k, rows(ch)]
    sends += list(home.values())

    gather = {}
    copies = []
    handed = {}
    for ch in range(CHUNKS):
        for dz in range(1, m):
            home[ch, dz].wait_recv()
        for j in range(mats):
            slot = place[j]
            picked[j, rows(ch)] = plane_in[ch][lax.div(slot, cap), lax.rem(slot, cap)]
        for d in range(1, chips):
            to = lax.rem(chip + d, chips)
            c = remote(
                picked.at[:, rows(ch)], out.at[:, core, chip, rows(ch)],
                s_out.at[ch, d], r_out.at[ch, d], at_chip(to),
            )
            c.start()
            gather[ch, d] = c
        c = remote(
            picked.at[:, rows(ch)], out.at[:, core, chip, rows(ch)],
            s_outf.at[ch, 0], r_outf.at[ch, 0], partner,
        )
        c.start()
        handed[ch, 0] = c
        c = pltpu.make_async_copy(
            picked.at[:, rows(ch)], out.at[:, core, chip, rows(ch)], local_sem.at[2 + ch]
        )
        c.start()
        copies.append(c)
    for ch in range(CHUNKS):
        for d in range(1, chips):
            gather[ch, d].wait_recv()
            source = lax.rem(chip + chips - d, chips)
            block = out.at[:, core, source, rows(ch)]
            c = remote(block, block, s_outf.at[ch, d], r_outf.at[ch, d], partner)
            c.start()
            handed[ch, d] = c
    for c in handed.values():
        c.wait_recv()
    sends += list(gather.values()) + list(handed.values())
    for c in copies:
        c.wait()
    for c in sends:
        c.wait_send()
    for d, c in guarded:

        @pl.when(d != 0)
        def _():
            c.wait_send()


def local(grads, proj, moment1, moment2, plan):
    n = lax.axis_size("dp")
    m = lax.axis_size("own")
    chips = n // 2
    mats, own_rows, cols = grads.shape[1:]
    cap, held_rows, rank = proj.shape[1:]
    rank_rows = moment1.shape[2]
    piece = held_rows // chips
    g = grads.reshape(mats, 2, chips, piece, cols)
    w = proj.reshape(cap, chips, piece, rank)
    vmem = pl.BlockSpec(memory_space=pltpu.VMEM)
    anywhere = pl.BlockSpec(memory_space=pl.ANY)
    dma = pltpu.SemaphoreType.DMA
    ch = CHUNKS
    share = (cap, rank_rows, cols)
    update, first, second = pl.pallas_call(
        functools.partial(kernel, n, m),
        out_shape=(
            jax.ShapeDtypeStruct(g.shape, BF16),
            jax.ShapeDtypeStruct(share, F32),
            jax.ShapeDtypeStruct(share, F32),
        ),
        in_specs=[pl.BlockSpec(memory_space=pltpu.SMEM), anywhere, anywhere, vmem, vmem],
        out_specs=(anywhere, vmem, vmem),
        scratch_shapes=[
            pltpu.VMEM((mats, chips, piece, cols), BF16),
            pltpu.VMEM((mats, chips, piece, cols), BF16),
            pltpu.VMEM((chips, mats, piece, cols), BF16),
            pltpu.VMEM((chips - 1, mats, piece, cols), BF16),
            pltpu.VMEM((mats, piece, cols), BF16),
            pltpu.VMEM((m - 1, cap, piece, cols), BF16),
            pltpu.VMEM((m, cap, piece, cols), BF16),
            pltpu.VMEM((cap, chips, piece, cols), BF16),
            pltpu.VMEM((cap, chips, piece, rank), BF16),
            pltpu.VMEM((2, cap, chips, rank_rows, cols), BF16),
            pltpu.VMEM((cap, chips, rank_rows, cols), BF16),
            pltpu.VMEM((cap, chips, rank_rows, cols), BF16),
            pltpu.VMEM((cap, chips - 1, rank_rows, cols), BF16),
            pltpu.VMEM((2 * cap, 1, cols), F32),
            pltpu.VMEM((n - 1, 2 * cap, 1, cols), F32),
            pltpu.VMEM((cap, n, rank_rows, cols), BF16),
            pltpu.VMEM((chips, cap, piece, cols), BF16),
            pltpu.VMEM((chips, cap, piece, cols), BF16),
            [pltpu.VMEM((m, cap, piece // ch, cols), BF16)] * ch,
            pltpu.VMEM((mats, piece, cols), BF16),
            dma((2 + ch,)),
            dma((ch,)), dma((ch,)),
            dma((ch, chips)), dma((ch, chips)),
            dma((ch, m)), dma((ch, m)),
            dma((ch, m)), dma((ch, chips)),
            dma((cap,)), dma((cap,)),
            dma((cap, chips)), dma((cap, chips)),
            dma((n,)), dma((n,)),
            dma((chips,)), dma((chips,)),
            dma((chips,)), dma((chips,)),
            dma((ch, chips)), dma((ch, chips)),
            dma((ch, m)), dma((ch, m)),
            dma((ch, chips)), dma((ch, chips)),
            dma((ch, chips)), dma((ch, chips)),
        ],
        compiler_params=pltpu.CompilerParams(collective_id=0, has_side_effects=True),
    )(plan, g, w, moment1[0], moment2[0])
    return (update.reshape(mats, own_rows, cols), first[None], second[None])


def solution(mesh):
    return jax.shard_map(
        local,
        mesh=mesh,
        in_specs=(
            P("dp", None, "own", None),
            P("own", None, "dp", None),
            P("own", None, "dp", None),
            P("own", None, "dp", None),
            P(),
        ),
        out_specs=(P(None, "own", None), P("own", None, "dp", None), P("own", None, "dp", None)),
        check_vma=False,
    )
```

```python
import functools
import jax
import jax.numpy as jnp
from jax import lax
from jax.experimental import pallas as pl
from jax.experimental.pallas import tpu as pltpu
from jax.sharding import PartitionSpec as P

beta_one = 0.9
beta_two = 0.999
adam_eps = 1e-08
norm_eps = 1e-06
correct_one = 1.0 - 0.9**10
correct_two = 1.0 - 0.999**10

CHUNKS = 4
F32 = jnp.float32
BF16 = jnp.bfloat16


def kernel(
    n, m, plan, grads, proj, m1, m2, out, m1_out, m2_out,
    own_half, pair_half, half_sum, chip_in, slot_out, slot_in, grad, weights,
    part, part_in, pair_sum, share_in, norms, norms_in, mixed, update, row_in, plane_in, picked,
    local_sem,
    s_pair, r_pair, s_chip, r_chip, s_slot, r_slot, s_row, r_row,
    s_part, r_part, s_share, r_share, s_norm, r_norm, s_mix, r_mix, s_mixf, r_mixf,
    s_back, r_back, s_home, r_home, s_out, r_out, s_outf, r_outf,
):
    mats = grads.shape[0]
    chips = n // 2
    piece = grads.shape[3]
    chunk = piece // CHUNKS
    cap = m1.shape[0]
    rank_rows = m1.shape[1]
    cols = m1.shape[2]
    rank = n * rank_rows
    dp = lax.axis_index("dp")
    own = lax.axis_index("own")
    core = lax.rem(dp, 2)
    chip = lax.div(dp, 2)
    other = 1 - core
    partner = (2 * chip + other, own)

    def at_chip(which):
        return (2 * which + core, own)

    def remote(src, dst, send, recv, device):
        return pltpu.make_async_remote_copy(
            src_ref=src, dst_ref=dst, send_sem=send, recv_sem=recv,
            device_id=device, device_id_type=pl.DeviceIdType.MESH,
        )

    bits = chips.bit_length() - 1

    def flip(which, mask):
        for b in range(bits):
            if mask >> b & 1:
                which = which + (1 << b) * (1 - 2 * lax.rem(lax.div(which, 1 << b), 2))
        return which

    groups = []
    for order, low, high in (
        (list(range(bits)), 0, mats // 2),
        (list(range(bits))[::-1], mats // 2, mats),
    ):
        groups.append((order, pl.ds(low, high - low)))

    def subsets(free):
        return [mask for mask in range(chips) if all(b in free for b in range(bits) if mask >> b & 1)]

    def rows(ch):
        return pl.ds(ch * chunk, chunk)

    load_half = pltpu.make_async_copy(grads.at[:, core], own_half, local_sem.at[0])
    load_half.start()
    load_proj = pltpu.make_async_copy(proj, weights, local_sem.at[1])
    load_proj.start()

    owner = [plan[j] for j in range(mats)]
    place = []
    for j in range(mats):
        before = jnp.int32(0)
        for i in range(j):
            before = before + jnp.where(owner[i] == owner[j], 1, 0)
        place.append(owner[j] * cap + before)

    def occupant(slot):
        index = jnp.int32(0)
        valid = jnp.int32(0)
        for j in range(mats):
            here = place[j] == slot
            index = jnp.where(here, j, index)
            valid = jnp.where(here, 1, valid)
        return index, valid.astype(F32)

    barrier = pltpu.get_barrier_semaphore()
    for d in range(1, n):
        pl.semaphore_signal(
            barrier, inc=1, device_id=(lax.rem(dp + d, n), own),
            device_id_type=pl.DeviceIdType.MESH,
        )
    for d in range(1, m):
        pl.semaphore_signal(
            barrier, inc=1, device_id=(dp, lax.rem(own + d, m)),
            device_id_type=pl.DeviceIdType.MESH,
        )
    pl.semaphore_wait(barrier, n - 1 + m - 1)

    sends = []

    pair = []
    for ch in range(CHUNKS):
        c = remote(
            grads.at[:, other, :, rows(ch)], pair_half.at[:, :, rows(ch)],
            s_pair.at[ch], r_pair.at[ch], partner,
        )
        c.start()
        pair.append(c)
    load_half.wait()
    over_chips = {}

    def send_chips(ch, at, step):
        order, span = groups[at]
        for mask in subsets(order[step + 1 :]):
            full = mask | 1 << order[step]
            c = remote(
                half_sum.at[full, span, rows(ch)], chip_in.at[step, mask, span, rows(ch)],
                s_chip.at[ch, at, full], r_chip.at[ch, at, full],
                at_chip(flip(chip, 1 << order[step])),
            )
            c.start()
            over_chips[ch, at, full] = c

    def take_chips(ch, at, step):
        order, span = groups[at]
        for mask in subsets(order[step + 1 :]):
            over_chips[ch, at, mask | 1 << order[step]].wait_recv()
            for j in range(span.start, span.start + span.size):
                value = half_sum[mask, j, rows(ch)].astype(F32) + chip_in[
                    step, mask, j, rows(ch)
                ].astype(F32)
                half_sum[mask, j, rows(ch)] = value.astype(BF16)

    for ch in range(CHUNKS):
        pair[ch].wait_recv()
        for mask in list(range(1, chips)) + [0]:
            t = flip(chip, mask)

            @pl.loop(0, mats)
            def _(j):
                half_sum[mask, j, rows(ch)] = (
                    own_half[j, t, rows(ch)].astype(F32) + pair_half[j, t, rows(ch)].astype(F32)
                ).astype(BF16)

        for at in range(2):
            send_chips(ch, at, 0)
    sends += pair

    to_owner = {}
    for ch in range(CHUNKS):
        for step in range(bits):
            for at in range(2):
                take_chips(ch, at, step)
                if step + 1 < bits:
                    send_chips(ch, at, step + 1)

        for dz in list(range(1, m)) + [0]:
            to = lax.rem(own + dz, m)
            for k in range(cap):
                index, valid = occupant(to * cap + k)
                value = (half_sum[0, index, rows(ch)].astype(F32) * valid).astype(BF16)
                if dz == 0:
                    slot_in[0, k, rows(ch)] = value
                else:
                    slot_out[dz - 1, k, rows(ch)] = value
            if dz > 0:
                c = remote(
                    slot_out.at[dz - 1, :, rows(ch)], slot_in.at[dz, :, rows(ch)],
                    s_slot.at[ch, dz], r_slot.at[ch, dz], (dp, to),
                )
                c.start()
                to_owner[ch, dz] = c
    sends += list(over_chips.values()) + list(to_owner.values())

    guarded = []
    for ch in range(CHUNKS):
        for dz in range(m):
            if dz > 0:
                to_owner[ch, dz].wait_recv()
            plane = lax.rem(own + m - dz, m)
            d = lax.rem(plane + chips - chip, chips)
            c = remote(
                slot_in.at[dz, :, rows(ch)], grad.at[:, chip, rows(ch)],
                s_row.at[ch, dz], r_row.at[ch, d], at_chip(plane),
            )

            @pl.when(d != 0)
            def _():
                c.start()

            @pl.when(d == 0)
            def _():
                for k in range(cap):
                    grad[k, chip, rows(ch)] = slot_in[dz, k, rows(ch)]

            guarded.append((d, c))
    for ch in range(CHUNKS):
        for d in range(1, chips):
            remote(
                slot_in.at[0, :, rows(ch)], grad.at[:, chip, rows(ch)],
                s_row.at[ch, 0], r_row.at[ch, d], at_chip(chip),
            ).wait_recv()

    load_proj.wait()
    parts = []
    for k in range(cap):
        g = grad[k].reshape(chips * piece, cols)
        w = weights[k].reshape(chips * piece, rank)
        value = lax.dot_general(g, w, (((0,), (0,)), ((), ())), preferred_element_type=F32)
        value = value.T.astype(BF16)
        for t in range(chips):
            for s in range(2):
                at = (2 * t + s) * rank_rows
                part[s, k, t] = value[at : at + rank_rows]
        c = remote(part.at[other, k], part_in.at[k], s_part.at[k], r_part.at[k], partner)
        c.start()
        parts.append(c)
    shares = {}
    for k in range(cap):
        parts[k].wait_recv()
        for t in range(chips):
            pair_sum[k, t] = (part[core, k, t].astype(F32) + part_in[k, t].astype(F32)).astype(BF16)
        for d in range(1, chips):
            to = lax.rem(chip + d, chips)
            c = remote(
                pair_sum.at[k, to], share_in.at[k, d - 1],
                s_share.at[k, d], r_share.at[k, d], at_chip(to),
            )
            c.start()
            shares[k, d] = c
    sends += parts + list(shares.values())

    rank_half = []
    adam = []
    for k in range(cap):
        for d in range(1, chips):
            shares[k, d].wait_recv()
        value = pair_sum[k, chip].astype(F32)
        for d in range(1, chips):
            value = value + share_in[k, d - 1].astype(F32)
        first = beta_one * m1[k] + (1.0 - beta_one) * value
        second = beta_two * m2[k] + (1.0 - beta_two) * value * value
        m1_out[k] = first
        m2_out[k] = second
        step = first / correct_one / (jnp.sqrt(second / correct_two) + adam_eps)
        step = step.astype(BF16)
        wide = step.astype(F32)
        norms[k] = jnp.sum(value * value, axis=0, keepdims=True)
        norms[cap + k] = jnp.sum(wide * wide, axis=0, keepdims=True)
        rank_half.append(value.astype(BF16))
        adam.append(wide)
    across = []
    for d in range(1, n):
        c = remote(
            norms, norms_in.at[d - 1], s_norm.at[d], r_norm.at[d], (lax.rem(dp + d, n), own)
        )
        c.start()
        across.append(c)
    sends += across
    for c in across:
        c.wait_recv()
    sums = norms[...]
    for d in range(1, n):
        sums = sums + norms_in[d - 1]
    scale = []
    for k in range(cap):
        scale.append(jnp.sqrt(sums[cap + k]) / (jnp.sqrt(sums[k]) + norm_eps))
        mixed[k, dp] = (adam[k] - scale[k] * rank_half[k].astype(F32)).astype(BF16)
    mix = []
    for d in range(1, chips):
        to = lax.rem(chip + d, chips)
        c = remote(mixed.at[:, dp], mixed.at[:, dp], s_mix.at[d], r_mix.at[d], at_chip(to))
        c.start()
        mix.append(c)
    forward = []
    c = remote(mixed.at[:, dp], mixed.at[:, dp], s_mixf.at[0], r_mixf.at[0], partner)
    c.start()
    forward.append(c)
    for d in range(1, chips):
        mix[d - 1].wait_recv()
        at = 2 * lax.rem(chip + chips - d, chips) + core
        c = remote(mixed.at[:, at], mixed.at[:, at], s_mixf.at[d], r_mixf.at[d], partner)
        c.start()
        forward.append(c)
    for c in forward:
        c.wait_recv()
    sends += mix + forward

    back = {}
    for ch in range(CHUNKS):
        for k in range(cap):
            w = weights[k, :, rows(ch)].reshape(chips * chunk, rank)
            c_full = mixed[k].reshape(rank, cols)
            value = jnp.dot(w, c_full, preferred_element_type=F32)
            g = grad[k, :, rows(ch)].reshape(chips * chunk, cols).astype(F32)
            value = (value + scale[k] * g).astype(BF16)
            for t in range(chips):
                update[t, k, rows(ch)] = value[t * chunk : (t + 1) * chunk]
        for k in range(cap):
            row_in[chip, k, rows(ch)] = update[chip, k, rows(ch)]
        for d in range(1, chips):
            to = lax.rem(chip + d, chips)
            c = remote(
                update.at[to, :, rows(ch)], row_in.at[chip, :, rows(ch)],
                s_back.at[ch, d], r_back.at[ch, d], at_chip(to),
            )
            c.start()
            back[ch, d] = c
    sends += list(back.values())

    home = {}
    for ch in range(CHUNKS):
        for d in range(1, chips):
            back[ch, d].wait_recv()
        for dz in range(1, m):
            to = lax.rem(own + dz, m)
            c = remote(
                row_in.at[to, :, rows(ch)], plane_in[ch].at[own],
                s_home.at[ch, dz], r_home.at[ch, dz], (dp, to),
            )
            c.start()
            home[ch, dz] = c
        for k in range(cap):
            plane_in[ch][own, k] = row_in[own, k, rows(ch)]
    sends += list(home.values())

    gather = {}
    copies = []
    handed = {}

    def send_gather(ch, at, step):
        order, span = groups[at]
        bit = 1 << order[step]
        for mask in subsets(order[:step]):
            block = out.at[span, core, flip(chip, mask), rows(ch)]
            source = picked.at[span, rows(ch)] if mask == 0 else block
            c = remote(
                source, block, s_out.at[ch, at, mask | bit], r_out.at[ch, at, mask | bit],
                at_chip(flip(chip, bit)),
            )
            c.start()
            gather[ch, at, mask | bit] = c

    def take_gather(ch, at, step):
        order, span = groups[at]
        bit = 1 << order[step]
        for mask in subsets(order[:step]):
            gather[ch, at, mask | bit].wait_recv()
        if step + 1 < bits:
            send_gather(ch, at, step + 1)
        for mask in subsets(order[:step]):
            block = out.at[span, core, flip(chip, mask | bit), rows(ch)]
            c = remote(
                block, block, s_outf.at[ch, at, mask | bit], r_outf.at[ch, at, mask | bit], partner
            )
            c.start()
            handed[ch, at, mask | bit] = c

    for ch in range(CHUNKS):
        for dz in range(1, m):
            home[ch, dz].wait_recv()
        for j in range(mats):
            slot = place[j]
            picked[j, rows(ch)] = plane_in[ch][lax.div(slot, cap), lax.rem(slot, cap)]
        for at in range(2):
            send_gather(ch, at, 0)
        for at in range(2):
            span = groups[at][1]
            c = remote(
                picked.at[span, rows(ch)], out.at[span, core, chip, rows(ch)],
                s_outf.at[ch, at, 0], r_outf.at[ch, at, 0], partner,
            )
            c.start()
            handed[ch, at, 0] = c
        c = pltpu.make_async_copy(
            picked.at[:, rows(ch)], out.at[:, core, chip, rows(ch)], local_sem.at[2 + ch]
        )
        c.start()
        copies.append(c)
        if ch > 0:
            for at in range(2):
                take_gather(ch - 1, at, 0)
    for at in range(2):
        take_gather(CHUNKS - 1, at, 0)
    for step in range(1, bits):
        for ch in range(CHUNKS):
            for at in range(2):
                take_gather(ch, at, step)
    for c in handed.values():
        c.wait_recv()
    sends += list(gather.values()) + list(handed.values())
    for c in copies:
        c.wait()
    for c in sends:
        c.wait_send()
    for d, c in guarded:

        @pl.when(d != 0)
        def _():
            c.wait_send()


def local(grads, proj, moment1, moment2, plan):
    n = lax.axis_size("dp")
    m = lax.axis_size("own")
    chips = n // 2
    mats, own_rows, cols = grads.shape[1:]
    cap, held_rows, rank = proj.shape[1:]
    rank_rows = moment1.shape[2]
    piece = held_rows // chips
    g = grads.reshape(mats, 2, chips, piece, cols)
    w = proj.reshape(cap, chips, piece, rank)
    vmem = pl.BlockSpec(memory_space=pltpu.VMEM)
    anywhere = pl.BlockSpec(memory_space=pl.ANY)
    dma = pltpu.SemaphoreType.DMA
    ch = CHUNKS
    bits = chips.bit_length() - 1
    share = (cap, rank_rows, cols)
    update, first, second = pl.pallas_call(
        functools.partial(kernel, n, m),
        out_shape=(
            jax.ShapeDtypeStruct(g.shape, BF16),
            jax.ShapeDtypeStruct(share, F32),
            jax.ShapeDtypeStruct(share, F32),
        ),
        in_specs=[pl.BlockSpec(memory_space=pltpu.SMEM), anywhere, anywhere, vmem, vmem],
        out_specs=(anywhere, vmem, vmem),
        scratch_shapes=[
            pltpu.VMEM((mats, chips, piece, cols), BF16),
            pltpu.VMEM((mats, chips, piece, cols), BF16),
            pltpu.VMEM((chips, mats, piece, cols), BF16),
            pltpu.VMEM((max(bits, 1), chips, mats, piece, cols), BF16),
            pltpu.VMEM((m - 1, cap, piece, cols), BF16),
            pltpu.VMEM((m, cap, piece, cols), BF16),
            pltpu.VMEM((cap, chips, piece, cols), BF16),
            pltpu.VMEM((cap, chips, piece, rank), BF16),
            pltpu.VMEM((2, cap, chips, rank_rows, cols), BF16),
            pltpu.VMEM((cap, chips, rank_rows, cols), BF16),
            pltpu.VMEM((cap, chips, rank_rows, cols), BF16),
            pltpu.VMEM((cap, chips - 1, rank_rows, cols), BF16),
            pltpu.VMEM((2 * cap, 1, cols), F32),
            pltpu.VMEM((n - 1, 2 * cap, 1, cols), F32),
            pltpu.VMEM((cap, n, rank_rows, cols), BF16),
            pltpu.VMEM((chips, cap, piece, cols), BF16),
            pltpu.VMEM((chips, cap, piece, cols), BF16),
            [pltpu.VMEM((m, cap, piece // ch, cols), BF16)] * ch,
            pltpu.VMEM((mats, piece, cols), BF16),
            dma((2 + ch,)),
            dma((ch,)), dma((ch,)),
            dma((ch, 2, chips)), dma((ch, 2, chips)),
            dma((ch, m)), dma((ch, m)),
            dma((ch, m)), dma((ch, chips)),
            dma((cap,)), dma((cap,)),
            dma((cap, chips)), dma((cap, chips)),
            dma((n,)), dma((n,)),
            dma((chips,)), dma((chips,)),
            dma((chips,)), dma((chips,)),
            dma((ch, chips)), dma((ch, chips)),
            dma((ch, m)), dma((ch, m)),
            dma((ch, 2, chips)), dma((ch, 2, chips)),
            dma((ch, 2, chips)), dma((ch, 2, chips)),
        ],
        compiler_params=pltpu.CompilerParams(collective_id=0, has_side_effects=True),
    )(plan, g, w, moment1[0], moment2[0])
    return (update.reshape(mats, own_rows, cols), first[None], second[None])


def solution(mesh):
    return jax.shard_map(
        local,
        mesh=mesh,
        in_specs=(
            P("dp", None, "own", None),
            P("own", None, "dp", None),
            P("own", None, "dp", None),
            P("own", None, "dp", None),
            P(),
        ),
        out_specs=(P(None, "own", None), P("own", None, "dp", None), P("own", None, "dp", None)),
        check_vma=False,
    )
```

```python
import functools
import jax
import jax.numpy as jnp
from jax import lax
from jax.experimental import pallas as pl
from jax.experimental.pallas import tpu as pltpu
from jax.sharding import PartitionSpec as P

beta_one = 0.9
beta_two = 0.999
adam_eps = 1e-08
norm_eps = 1e-06
correct_one = 1.0 - 0.9**10
correct_two = 1.0 - 0.999**10

CHUNKS = 4
F32 = jnp.float32
BF16 = jnp.bfloat16


def kernel(
    n, m, plan, grads, proj, m1, m2, out, m1_out, m2_out,
    own_half, pair_half, half_sum, chip_in, total, slot_out, slot_in, grad, weights,
    part, part_in, pair_sum, share_in, norms, norms_in, mixed, update, row_in, plane_in, picked,
    local_sem,
    s_pair, r_pair, s_chip, r_chip, s_slot, r_slot, s_row, r_row,
    s_part, r_part, s_share, r_share, s_norm, r_norm, s_mix, r_mix, s_mixf, r_mixf,
    s_back, r_back, s_home, r_home, s_out, r_out, s_outf, r_outf,
):
    mats = grads.shape[0]
    chips = n // 2
    piece = grads.shape[3]
    chunk = piece // CHUNKS
    cap = m1.shape[0]
    rank_rows = m1.shape[1]
    cols = m1.shape[2]
    rank = n * rank_rows
    dp = lax.axis_index("dp")
    own = lax.axis_index("own")
    core = lax.rem(dp, 2)
    chip = lax.div(dp, 2)
    other = 1 - core
    partner = (2 * chip + other, own)

    def at_chip(which):
        return (2 * which + core, own)

    def remote(src, dst, send, recv, device):
        return pltpu.make_async_remote_copy(
            src_ref=src, dst_ref=dst, send_sem=send, recv_sem=recv,
            device_id=device, device_id_type=pl.DeviceIdType.MESH,
        )

    def rows(ch):
        return pl.ds(ch * chunk, chunk)

    load_half = pltpu.make_async_copy(grads.at[:, core], own_half, local_sem.at[0])
    load_half.start()
    load_proj = pltpu.make_async_copy(proj, weights, local_sem.at[1])
    load_proj.start()

    owner = [plan[j] for j in range(mats)]
    place = []
    for j in range(mats):
        before = jnp.int32(0)
        for i in range(j):
            before = before + jnp.where(owner[i] == owner[j], 1, 0)
        place.append(owner[j] * cap + before)

    def occupant(slot):
        index = jnp.int32(0)
        valid = jnp.int32(0)
        for j in range(mats):
            here = place[j] == slot
            index = jnp.where(here, j, index)
            valid = jnp.where(here, 1, valid)
        return index, valid.astype(F32)

    barrier = pltpu.get_barrier_semaphore()
    for d in range(1, n):
        pl.semaphore_signal(
            barrier, inc=1, device_id=(lax.rem(dp + d, n), own),
            device_id_type=pl.DeviceIdType.MESH,
        )
    for d in range(1, m):
        pl.semaphore_signal(
            barrier, inc=1, device_id=(dp, lax.rem(own + d, m)),
            device_id_type=pl.DeviceIdType.MESH,
        )
    pl.semaphore_wait(barrier, n - 1 + m - 1)

    sends = []

    pair = []
    for ch in range(CHUNKS):
        c = remote(
            grads.at[:, other, :, rows(ch)], pair_half.at[:, :, rows(ch)],
            s_pair.at[ch], r_pair.at[ch], partner,
        )
        c.start()
        pair.append(c)
    load_half.wait()
    over_chips = {}
    for ch in range(CHUNKS):
        pair[ch].wait_recv()

        @pl.loop(0, mats * chips)
        def _(i):
            j = lax.div(i, chips)
            t = lax.rem(i, chips)
            half_sum[t, j, rows(ch)] = (
                own_half[j, t, rows(ch)].astype(F32) + pair_half[j, t, rows(ch)].astype(F32)
            ).astype(BF16)

        for d in range(1, chips):
            to = lax.rem(chip + d, chips)
            c = remote(
                half_sum.at[to, :, rows(ch)], chip_in.at[d - 1, :, rows(ch)],
                s_chip.at[ch, d], r_chip.at[ch, d], at_chip(to),
            )
            c.start()
            over_chips[ch, d] = c
    sends += pair + list(over_chips.values())

    to_owner = {}
    for ch in range(CHUNKS):
        for d in range(1, chips):
            over_chips[ch, d].wait_recv()

        @pl.loop(0, mats)
        def _(j):
            acc = half_sum[chip, j, rows(ch)].astype(F32)
            for d in range(1, chips):
                acc = acc + chip_in[d - 1, j, rows(ch)].astype(F32)
            total[j, rows(ch)] = acc.astype(BF16)

        for dz in list(range(1, m)) + [0]:
            to = lax.rem(own + dz, m)
            for k in range(cap):
                index, valid = occupant(to * cap + k)
                value = (total[index, rows(ch)].astype(F32) * valid).astype(BF16)
                if dz == 0:
                    slot_in[0, k, rows(ch)] = value
                else:
                    slot_out[dz - 1, k, rows(ch)] = value
            if dz > 0:
                c = remote(
                    slot_out.at[dz - 1, :, rows(ch)], slot_in.at[dz, :, rows(ch)],
                    s_slot.at[ch, dz], r_slot.at[ch, dz], (dp, to),
                )
                c.start()
                to_owner[ch, dz] = c
    sends += list(to_owner.values())

    guarded = []
    for ch in range(CHUNKS):
        for dz in range(m):
            if dz > 0:
                to_owner[ch, dz].wait_recv()
            plane = lax.rem(own + m - dz, m)
            d = lax.rem(plane + chips - chip, chips)
            c = remote(
                slot_in.at[dz, :, rows(ch)], grad.at[:, chip, rows(ch)],
                s_row.at[ch, dz], r_row.at[ch, d], at_chip(plane),
            )

            @pl.when(d != 0)
            def _():
                c.start()

            @pl.when(d == 0)
            def _():
                for k in range(cap):
                    grad[k, chip, rows(ch)] = slot_in[dz, k, rows(ch)]

            guarded.append((d, c))
    for ch in range(CHUNKS):
        for d in range(1, chips):
            remote(
                slot_in.at[0, :, rows(ch)], grad.at[:, chip, rows(ch)],
                s_row.at[ch, 0], r_row.at[ch, d], at_chip(chip),
            ).wait_recv()

    load_proj.wait()
    parts = []
    for k in range(cap):
        g = grad[k].reshape(chips * piece, cols)
        w = weights[k].reshape(chips * piece, rank)
        value = lax.dot_general(g, w, (((0,), (0,)), ((), ())), preferred_element_type=F32)
        value = value.T.astype(BF16)
        for t in range(chips):
            for s in range(2):
                at = (2 * t + s) * rank_rows
                part[s, k, t] = value[at : at + rank_rows]
        c = remote(part.at[other, k], part_in.at[k], s_part.at[k], r_part.at[k], partner)
        c.start()
        parts.append(c)
    shares = {}
    for k in range(cap):
        parts[k].wait_recv()
        for t in range(chips):
            pair_sum[k, t] = (part[core, k, t].astype(F32) + part_in[k, t].astype(F32)).astype(BF16)
        for d in range(1, chips):
            to = lax.rem(chip + d, chips)
            c = remote(
                pair_sum.at[k, to], share_in.at[k, d - 1],
                s_share.at[k, d], r_share.at[k, d], at_chip(to),
            )
            c.start()
            shares[k, d] = c
    sends += parts + list(shares.values())

    rank_half = []
    adam = []
    for k in range(cap):
        for d in range(1, chips):
            shares[k, d].wait_recv()
        value = pair_sum[k, chip].astype(F32)
        for d in range(1, chips):
            value = value + share_in[k, d - 1].astype(F32)
        first = beta_one * m1[k] + (1.0 - beta_one) * value
        second = beta_two * m2[k] + (1.0 - beta_two) * value * value
        m1_out[k] = first
        m2_out[k] = second
        step = first / correct_one / (jnp.sqrt(second / correct_two) + adam_eps)
        step = step.astype(BF16)
        wide = step.astype(F32)
        norms[k] = jnp.sum(value * value, axis=0, keepdims=True)
        norms[cap + k] = jnp.sum(wide * wide, axis=0, keepdims=True)
        rank_half.append(value.astype(BF16))
        adam.append(wide)
    across = []
    for d in range(1, n):
        c = remote(
            norms, norms_in.at[d - 1], s_norm.at[d], r_norm.at[d], (lax.rem(dp + d, n), own)
        )
        c.start()
        across.append(c)
    sends += across
    for c in across:
        c.wait_recv()
    sums = norms[...]
    for d in range(1, n):
        sums = sums + norms_in[d - 1]
    scale = []
    for k in range(cap):
        scale.append(jnp.sqrt(sums[cap + k]) / (jnp.sqrt(sums[k]) + norm_eps))
        mixed[k, dp] = (adam[k] - scale[k] * rank_half[k].astype(F32)).astype(BF16)
    mix = []
    for d in range(1, chips):
        to = lax.rem(chip + d, chips)
        c = remote(mixed.at[:, dp], mixed.at[:, dp], s_mix.at[d], r_mix.at[d], at_chip(to))
        c.start()
        mix.append(c)
    forward = []
    c = remote(mixed.at[:, dp], mixed.at[:, dp], s_mixf.at[0], r_mixf.at[0], partner)
    c.start()
    forward.append(c)
    for d in range(1, chips):
        mix[d - 1].wait_recv()
        at = 2 * lax.rem(chip + chips - d, chips) + core
        c = remote(mixed.at[:, at], mixed.at[:, at], s_mixf.at[d], r_mixf.at[d], partner)
        c.start()
        forward.append(c)
    for c in forward:
        c.wait_recv()
    sends += mix + forward

    back = {}
    for ch in range(CHUNKS):
        for k in range(cap):
            w = weights[k, :, rows(ch)].reshape(chips * chunk, rank)
            c_full = mixed[k].reshape(rank, cols)
            value = jnp.dot(w, c_full, preferred_element_type=F32)
            g = grad[k, :, rows(ch)].reshape(chips * chunk, cols).astype(F32)
            value = (value + scale[k] * g).astype(BF16)
            for t in range(chips):
                update[t, k, rows(ch)] = value[t * chunk : (t + 1) * chunk]
        for k in range(cap):
            row_in[chip, k, rows(ch)] = update[chip, k, rows(ch)]
        for d in range(1, chips):
            to = lax.rem(chip + d, chips)
            c = remote(
                update.at[to, :, rows(ch)], row_in.at[chip, :, rows(ch)],
                s_back.at[ch, d], r_back.at[ch, d], at_chip(to),
            )
            c.start()
            back[ch, d] = c
    sends += list(back.values())

    home = {}
    for ch in range(CHUNKS):
        for d in range(1, chips):
            back[ch, d].wait_recv()
        for dz in range(1, m):
            to = lax.rem(own + dz, m)
            c = remote(
                row_in.at[to, :, rows(ch)], plane_in[ch].at[own],
                s_home.at[ch, dz], r_home.at[ch, dz], (dp, to),
            )
            c.start()
            home[ch, dz] = c
        for k in range(cap):
            plane_in[ch][own, k] = row_in[own, k, rows(ch)]
    sends += list(home.values())

    gather = {}
    copies = []
    handed = {}
    for ch in range(CHUNKS):
        for dz in range(1, m):
            home[ch, dz].wait_recv()
        for j in range(mats):
            slot = place[j]
            picked[j, rows(ch)] = plane_in[ch][lax.div(slot, cap), lax.rem(slot, cap)]
        for d in range(1, chips):
            to = lax.rem(chip + d, chips)
            c = remote(
                picked.at[:, rows(ch)], out.at[:, core, chip, rows(ch)],
                s_out.at[ch, d], r_out.at[ch, d], at_chip(to),
            )
            c.start()
            gather[ch, d] = c
        c = remote(
            picked.at[:, rows(ch)], out.at[:, core, chip, rows(ch)],
            s_outf.at[ch, 0], r_outf.at[ch, 0], partner,
        )
        c.start()
        handed[ch, 0] = c
        c = pltpu.make_async_copy(
            picked.at[:, rows(ch)], out.at[:, core, chip, rows(ch)], local_sem.at[2 + ch]
        )
        c.start()
        copies.append(c)
    for ch in range(CHUNKS):
        for d in range(1, chips):
            gather[ch, d].wait_recv()
            source = lax.rem(chip + chips - d, chips)
            block = out.at[:, core, source, rows(ch)]
            c = remote(block, block, s_outf.at[ch, d], r_outf.at[ch, d], partner)
            c.start()
            handed[ch, d] = c
    for c in handed.values():
        c.wait_recv()
    sends += list(gather.values()) + list(handed.values())
    for c in copies:
        c.wait()
    for c in sends:
        c.wait_send()
    for d, c in guarded:

        @pl.when(d != 0)
        def _():
            c.wait_send()


def local(grads, proj, moment1, moment2, plan):
    n = lax.axis_size("dp")
    m = lax.axis_size("own")
    chips = n // 2
    mats, own_rows, cols = grads.shape[1:]
    cap, held_rows, rank = proj.shape[1:]
    rank_rows = moment1.shape[2]
    piece = held_rows // chips
    g = grads.reshape(mats, 2, chips, piece, cols)
    w = proj.reshape(cap, chips, piece, rank)
    vmem = pl.BlockSpec(memory_space=pltpu.VMEM)
    anywhere = pl.BlockSpec(memory_space=pl.ANY)
    dma = pltpu.SemaphoreType.DMA
    ch = CHUNKS
    share = (cap, rank_rows, cols)
    update, first, second = pl.pallas_call(
        functools.partial(kernel, n, m),
        out_shape=(
            jax.ShapeDtypeStruct(g.shape, BF16),
            jax.ShapeDtypeStruct(share, F32),
            jax.ShapeDtypeStruct(share, F32),
        ),
        in_specs=[pl.BlockSpec(memory_space=pltpu.SMEM), anywhere, anywhere, vmem, vmem],
        out_specs=(anywhere, vmem, vmem),
        scratch_shapes=[
            pltpu.VMEM((mats, chips, piece, cols), BF16),
            pltpu.VMEM((mats, chips, piece, cols), BF16),
            pltpu.VMEM((chips, mats, piece, cols), BF16),
            pltpu.VMEM((chips - 1, mats, piece, cols), BF16),
            pltpu.VMEM((mats, piece, cols), BF16),
            pltpu.VMEM((m - 1, cap, piece, cols), BF16),
            pltpu.VMEM((m, cap, piece, cols), BF16),
            pltpu.VMEM((cap, chips, piece, cols), BF16),
            pltpu.VMEM((cap, chips, piece, rank), BF16),
            pltpu.VMEM((2, cap, chips, rank_rows, cols), BF16),
            pltpu.VMEM((cap, chips, rank_rows, cols), BF16),
            pltpu.VMEM((cap, chips, rank_rows, cols), BF16),
            pltpu.VMEM((cap, chips - 1, rank_rows, cols), BF16),
            pltpu.VMEM((2 * cap, 1, cols), F32),
            pltpu.VMEM((n - 1, 2 * cap, 1, cols), F32),
            pltpu.VMEM((cap, n, rank_rows, cols), BF16),
            pltpu.VMEM((chips, cap, piece, cols), BF16),
            pltpu.VMEM((chips, cap, piece, cols), BF16),
            [pltpu.VMEM((m, cap, piece // ch, cols), BF16)] * ch,
            pltpu.VMEM((mats, piece, cols), BF16),
            dma((2 + ch,)),
            dma((ch,)), dma((ch,)),
            dma((ch, chips)), dma((ch, chips)),
            dma((ch, m)), dma((ch, m)),
            dma((ch, m)), dma((ch, chips)),
            dma((cap,)), dma((cap,)),
            dma((cap, chips)), dma((cap, chips)),
            dma((n,)), dma((n,)),
            dma((chips,)), dma((chips,)),
            dma((chips,)), dma((chips,)),
            dma((ch, chips)), dma((ch, chips)),
            dma((ch, m)), dma((ch, m)),
            dma((ch, chips)), dma((ch, chips)),
            dma((ch, chips)), dma((ch, chips)),
        ],
        compiler_params=pltpu.CompilerParams(collective_id=0, has_side_effects=True),
    )(plan, g, w, moment1[0], moment2[0])
    return (update.reshape(mats, own_rows, cols), first[None], second[None])


def solution(mesh):
    return jax.shard_map(
        local,
        mesh=mesh,
        in_specs=(
            P("dp", None, "own", None),
            P("own", None, "dp", None),
            P("own", None, "dp", None),
            P("own", None, "dp", None),
            P(),
        ),
        out_specs=(P(None, "own", None), P("own", None, "dp", None), P("own", None, "dp", None)),
        check_vma=False,
    )
```
